256 devices in a mesh: leaf: 64 (over y, z, core), front: 4 (over x).
Axes of the slice: x: 4, y: 4, z: 8, core: 2. Of those that a mesh axis runs over, the one named last changes fastest.
Arguments:
- rhs_sub: float32 [8, 524288], P(None, ('leaf', 'front')), may hold values from -6 to 6
- rhs_sep: float32 [8, 16384], P(None, 'leaf'), may hold values from -6 to 6
- live_rows: int32 [256], P(('leaf', 'front')), may hold values from 256 to 2048, as said below
- lower_inv: bfloat16 [2048, 256, 256], P(('leaf', 'front')), as said below
- upper_inv: bfloat16 [2048, 256, 256], P(('leaf', 'front'))
- couple_low: bfloat16 [16384, 16384], P(('leaf', 'front')), may hold values from -0.1875 to 0.1875
- couple_up: bfloat16 [16384, 16384], P(('leaf', 'front')), may hold values from -0.046875 to 0.046875
- sep_lower_inv: bfloat16 [16384, 16384], P('leaf', 'front')
- sep_upper_inv: bfloat16 [16384, 16384], P('leaf', 'front')
- basis_sub: float32 [48, 524288], P(None, ('leaf', 'front')), may hold values from -0.0078125 to 0.0078125
- basis_sep: float32 [48, 16384], P(None, 'leaf'), may hold values from -0.0078125 to 0.0078125
Outputs:
- orth_sub: float32 [8, 524288], P(None, ('leaf', 'front'))
- orth_sep: float32 [8, 16384], P(None, 'leaf')
- coef: float32 [48, 8], replicated
The draws below stay inside these ranges and needn't reach their ends.
Inputs may be any that keep to these rules, and one draw needn't show every extreme that they name: `live_rows`: each entry is a multiple of 256; some device has all 2048 rows live. Every block of lower_inv is lower triangular, and every block of upper_inv, sep_lower_inv and sep_upper_inv upper triangular, each with a diagonal between 1 and 1.5.
All inputs are finite; a program needn't handle non-finite values.
Results may differ from the reference program's by a relative error of at most 0.0055.
Values may be sent and summed in bfloat16 or wider, within the bound.
No kernel may reach another device: no remote copies, remote signals or barrier semaphores. Data moves between devices by JAX's collectives and lax.ppermute only.
A program may use at most 64 MiB of HBM per device.

```python
import math
import jax
import jax.numpy as jnp
from jax import lax

VECS = 8
BASIS = 48
FRONT_ROWS = 256
BORDER = 64
SEP = 16384
ROWS_DEV = 2048
FRONTS = 8
TOTAL_ROWS = 524288
DEVICES = 256


def triangle(seed_key, block_count, size_order, upper_side):
    positions = jnp.arange(size_order)
    if upper_side:
        kept_part = positions[None, :] >= positions[:, None]
    else:
        kept_part = positions[None, :] <= positions[:, None]
    values = jax.random.normal(seed_key, (block_count, size_order, size_order), jnp.float32)
    values = values * (1.0 / math.sqrt(size_order))
    diagonal = 1.0 + 0.5 * jax.random.uniform(jax.random.fold_in(seed_key, 3), (block_count, size_order, 1), jnp.float32)
    on_diagonal = positions[None, :] == positions[:, None]
    return jnp.where(on_diagonal, diagonal, jnp.where(kept_part, values, 0.0))


def draw_live_rows(key, part):
    tiles = jax.random.randint(key, (DEVICES,), 1, FRONTS + 1) * FRONT_ROWS
    chosen = jax.random.randint(jax.random.fold_in(key, 7), (), 0, DEVICES)
    return jnp.where(jnp.arange(DEVICES) == chosen, ROWS_DEV, tiles).astype(jnp.int32)


def draw_lower_inv(key, part):
    return triangle(jax.random.fold_in(key, 11), DEVICES * FRONTS, FRONT_ROWS, False).astype(jnp.bfloat16)


def draw_upper_inv(key, part):
    return triangle(jax.random.fold_in(key, 12), DEVICES * FRONTS, FRONT_ROWS, True).astype(jnp.bfloat16)


def draw_sep_lower_inv(key, part):
    return triangle(jax.random.fold_in(key, 13), 1, SEP, True).reshape(SEP, SEP).astype(jnp.bfloat16)


def draw_sep_upper_inv(key, part):
    return triangle(jax.random.fold_in(key, 14), 1, SEP, True).reshape(SEP, SEP).astype(jnp.bfloat16)


def raised(result, stream_key, source, target, blocks, factor):
    def block_of(position):
        return (jnp.arange(result.shape[position]) // (result.shape[position] // blocks)).reshape((-1,) + (1,) * (result.ndim - 1 - position))

    first = jax.random.permutation(stream_key, blocks)[block_of(target)]
    second = (block_of(target) + blocks // 2) % blocks
    return jnp.where((block_of(source) == first) | (block_of(source) == second), factor * result, result)


def block_scale(stream_key, shape, pieces, smallest, largest):
    level, own = 1.0, jax.random.fold_in(stream_key, 6)
    for position, parts in pieces:
        draws = jnp.exp(jax.random.uniform(jax.random.fold_in(own, position), (parts,), jnp.float32, smallest / len(pieces), largest / len(pieces)))
        level = level * jnp.repeat(draws, shape[position] // parts).reshape([-1 if axis == position else 1 for axis in range(len(shape))])
    return level


def centred(own_key, dims, width, reach, pieces=(), held_as=jnp.bfloat16):
    level = block_scale(own_key, dims, pieces, -0.22, 0.18) if pieces else 1.0
    array = jax.random.normal(own_key, dims, jnp.float32) * width * level
    return jnp.minimum(jnp.maximum(array, -reach), reach).astype(held_as)


def bell_draw_with(own_key, shape, spread, most, shards, heavy, kind=jnp.bfloat16):
    entries = spread * jax.random.normal(own_key, shape, jnp.float32)
    if shards:
        entries = entries * block_scale(own_key, shape, shards, -0.22, 0.18)
    return jnp.clip(raised(entries, jax.random.fold_in(own_key, 3), *heavy), -most, most).astype(kind)


def setup_inputs(seed: int = 0) -> dict:
    splits = jax.random.split(jax.random.key(seed), 12)
    return {
        "rhs_sub": centred(splits[0], (VECS, TOTAL_ROWS), 1.0, 6.0, ((1, 256),), jnp.float32),
        "rhs_sep": centred(splits[1], (VECS, SEP), 1.0, 6.0, ((1, 64),), jnp.float32),
        "live_rows": draw_live_rows(jax.random.fold_in(splits[11], 71), 0),
        "lower_inv": draw_lower_inv(jax.random.fold_in(splits[11], 71), 0),
        "upper_inv": draw_upper_inv(jax.random.fold_in(splits[11], 71), 0),
        "couple_low": bell_draw_with(splits[5], (DEVICES * BORDER, SEP), (DEVICES * BORDER) ** -0.5, 0.1875, ((0, 256),), (0, 1, 256, 6.0)),
        "couple_up": centred(splits[6], (DEVICES * BORDER, SEP), SEP ** -0.5, 0.046875, ((0, 256),)),
        "sep_lower_inv": draw_sep_lower_inv(jax.random.fold_in(splits[11], 71), 0),
        "sep_upper_inv": draw_sep_upper_inv(jax.random.fold_in(splits[11], 71), 0),
        "basis_sub": centred(splits[9], (BASIS, TOTAL_ROWS), (TOTAL_ROWS + SEP) ** -0.5, 0.0078125, ((1, 256),), jnp.float32),
        "basis_sep": centred(splits[10], (BASIS, SEP), (TOTAL_ROWS + SEP) ** -0.5, 0.0078125, ((1, 64),), jnp.float32),
    }


def apply_blocks(vectors, inverse):
    vec_count = vectors.shape[0]
    shaped = vectors.astype(jnp.bfloat16).astype(jnp.float32).reshape(vec_count, inverse.shape[0], inverse.shape[1])
    product = jnp.einsum("vkr,krc->vkc", shaped, inverse.astype(jnp.float32))
    return product.reshape(vec_count, inverse.shape[0] * inverse.shape[2])


def reference(rhs_sub, rhs_sep, live_rows, lower_inv, upper_inv, couple_low, couple_up, sep_lower_inv, sep_upper_inv, basis_sub, basis_sep):
    vec_count = rhs_sub.shape[0]
    row_number = jnp.arange(ROWS_DEV, dtype=jnp.int32)
    live_mask = (row_number[None, :] < live_rows[:, None]).reshape(1, DEVICES * ROWS_DEV)
    lower_sol = jnp.where(live_mask, apply_blocks(rhs_sub, lower_inv), 0.0)
    per_device = lower_sol.reshape(vec_count, DEVICES, ROWS_DEV)
    border_rows = per_device[:, :, :BORDER].reshape(vec_count, DEVICES * BORDER).astype(jnp.bfloat16)
    top_rhs = rhs_sep - jnp.dot(border_rows, couple_low, preferred_element_type=jnp.float32)
    top_lower = jnp.dot(top_rhs.astype(jnp.bfloat16), sep_lower_inv, preferred_element_type=jnp.float32)
    top_sol = lax.dot_general(top_lower.astype(jnp.bfloat16), sep_upper_inv, (((1,), (1,)), ((), ())), preferred_element_type=jnp.float32)
    correction = lax.dot_general(top_sol.astype(jnp.bfloat16), couple_up, (((1,), (1,)), ((), ())), preferred_element_type=jnp.float32)
    correction = correction.reshape(vec_count, DEVICES, BORDER)
    updated = jnp.concatenate([per_device[:, :, :BORDER] - correction, per_device[:, :, BORDER:]], axis=2)
    updated = updated.reshape(vec_count, DEVICES * ROWS_DEV)
    upper_sol = jnp.where(live_mask, apply_blocks(updated, upper_inv), 0.0)
    coef_sum = jnp.zeros((BASIS, vec_count), jnp.float32)
    high = lax.Precision.HIGHEST
    for sweep in range(2):
        coef_pass = jnp.dot(basis_sub, upper_sol.T, precision=high) + jnp.dot(basis_sep, top_sol.T, precision=high)
        upper_sol = upper_sol - jnp.dot(coef_pass.T, basis_sub, precision=high)
        top_sol = top_sol - jnp.dot(coef_pass.T, basis_sep, precision=high)
        coef_sum = coef_sum + coef_pass
    return (upper_sol, top_sol, coef_sum)
```

```python
import jax
import jax.numpy as jnp
from jax import lax
from jax.sharding import Mesh, PartitionSpec as P

HIGH = lax.Precision.HIGHEST
F32 = jnp.float32
BF16 = jnp.bfloat16
YZ = ("y", "z")


def swap_core(value):
    return lax.ppermute(value, "c", [(0, 1), (1, 0)])


def sum_front(value):
    count = lax.axis_size("x")
    moved = [
        lax.ppermute(value, "x", [(i, (i + step) % count) for i in range(count)])
        for step in range(1, count)
    ]
    for other in moved:
        value = value + other
    return value


def exchange(value):
    return lax.all_to_all(value, YZ, 0, 0, tiled=True)


def to_tiles(value, count):
    rows, cols = value.shape
    return value.reshape(rows, count, cols // count).transpose(1, 0, 2)


def from_tiles(value):
    count, rows, cols = value.shape
    return value.transpose(1, 0, 2).reshape(rows, count * cols)


def shards(
    rhs_sub,
    rhs_sep,
    live_rows,
    lower_inv,
    upper_inv,
    couple_low,
    couple_up,
    sep_lower_inv,
    sep_upper_inv,
    basis_sub,
    basis_sep,
):
    vecs, rows = rhs_sub.shape
    blocks, block, _ = lower_inv.shape
    border = couple_low.shape[0]
    basis = basis_sub.shape[0]
    own = rhs_sep.shape[1]
    group = lax.axis_size("y") * lax.axis_size("z")
    front = lax.axis_size("x")
    core = lax.axis_index("c")

    shaped = rhs_sub.astype(BF16).reshape(vecs, blocks, block)
    first = jnp.dot(shaped[:, 0], lower_inv[0], preferred_element_type=F32)
    border_rows = first[:, :border].astype(BF16)
    part = jnp.dot(border_rows, couple_low, preferred_element_type=F32).astype(BF16)
    got = exchange(to_tiles(part, group)).astype(F32).sum(0)
    got = got + swap_core(got)
    got = jnp.where(core == 0, got[:, :own], got[:, own:])
    top_rhs = rhs_sep - sum_front(got)

    gram = lax.dot_general(basis_sub, basis_sub, (((1,), (1,)), ((), ())), precision=HIGH)
    gram = gram + (1.0 / front) * lax.dot_general(
        basis_sep, basis_sep, (((1,), (1,)), ((), ())), precision=HIGH
    )
    lanes = sep_lower_inv.shape[1] // group
    gram = jnp.pad(gram, ((0, group * vecs - basis), (0, lanes - basis)))
    gram = gram.reshape(group, vecs, lanes)

    lower_part = jnp.dot(top_rhs.astype(BF16), sep_lower_inv, preferred_element_type=F32)
    pack = jnp.concatenate([to_tiles(lower_part, group), gram], axis=2)
    got = exchange(pack).sum(0)
    got = got + swap_core(got)
    gram_tile = got[:, lanes:]
    mine = got[:, :lanes].astype(BF16)
    top_lower = from_tiles(exchange(jnp.broadcast_to(mine[None], (group,) + mine.shape)))
    upper_part = lax.dot_general(
        top_lower, sep_upper_inv, (((1,), (1,)), ((), ())), preferred_element_type=F32
    )
    got = sum_front(jnp.concatenate([upper_part, gram_tile], axis=1))
    top_sol = got[:, :own]
    gram_tile = got[:, own:]

    mine = top_sol.astype(BF16)
    other = swap_core(mine)
    pair = jnp.concatenate(
        [jnp.where(core == 0, mine, other), jnp.where(core == 0, other, mine)], axis=1
    )
    full = from_tiles(exchange(jnp.broadcast_to(pair[None], (group,) + pair.shape)))
    correction = lax.dot_general(
        full, couple_up, (((1,), (1,)), ((), ())), preferred_element_type=F32
    )

    live = lax.broadcasted_iota(jnp.int32, (1, blocks, 1), 1) * block < live_rows[0]
    lower = jnp.einsum("vkr,krc->vkc", shaped, lower_inv, preferred_element_type=F32)
    lower = jnp.where(live, lower, 0.0)
    upper = jnp.einsum("vkr,krc->vkc", lower.astype(BF16)[:, 1:], upper_inv[1:], preferred_element_type=F32)
    upper = jnp.where(live[:, 1:], upper, 0.0).reshape(vecs, rows - block)
    updated = jnp.concatenate([first[:, :border] - correction, first[:, border:]], axis=1)
    head = jnp.dot(updated.astype(BF16), upper_inv[0], preferred_element_type=F32)
    upper_sol = jnp.concatenate([head, upper], axis=1)

    coef = lax.dot_general(upper_sol, basis_sub, (((1,), (1,)), ((), ())), precision=HIGH)
    coef = coef + (1.0 / front) * lax.dot_general(
        top_sol, basis_sep, (((1,), (1,)), ((), ())), precision=HIGH
    )
    pack = jnp.concatenate(
        [jnp.pad(coef, ((0, 0), (0, lanes // 2 - basis))), gram_tile[:, : lanes // 2]], axis=1
    )
    got = exchange(jnp.broadcast_to(pack[None], (group,) + pack.shape))
    coef = got[:, :, :basis].sum(0)
    coef = sum_front(coef + swap_core(coef))
    gram = got[: basis // vecs, :, lanes // 2 : lanes // 2 + basis].reshape(basis, basis)
    coef = 2.0 * coef - jnp.dot(coef, gram, precision=HIGH)
    orth_sub = upper_sol - jnp.dot(coef, basis_sub, precision=HIGH)
    orth_sep = top_sol - jnp.dot(coef, basis_sep, precision=HIGH)
    return (orth_sub, orth_sep, coef.T)


def solution(mesh):
    split = Mesh(mesh.devices.reshape(4, 8, 2, 4), ("y", "z", "c", "x"))
    leaf = ("y", "z", "c")
    every = ("y", "z", "c", "x")
    return jax.shard_map(
        shards,
        mesh=split,
        in_specs=(
            P(None, every),
            P(None, leaf),
            P(every),
            P(every, None, None),
            P(every, None, None),
            P(every, None),
            P(every, None),
            P(leaf, "x"),
            P(leaf, "x"),
            P(None, every),
            P(None, leaf),
        ),
        out_specs=(P(None, every), P(None, leaf), P()),
        check_vma=False,
    )
```

```python
import functools

import jax
import jax.numpy as jnp
from jax import lax
from jax.experimental import pallas as pl
from jax.experimental.pallas import tpu as pltpu
from jax.sharding import Mesh, PartitionSpec as P

HIGH = lax.Precision.HIGHEST
F32 = jnp.float32
BF16 = jnp.bfloat16
YZ = ("y", "z")
CX = ("c", "x")
BY_LAST = (((1,), (1,)), ((), ()))


def swap_core(value):
    return lax.ppermute(value, "c", [(0, 1), (1, 0)])


def exchange(value, axes):
    return lax.all_to_all(value, axes, 0, 0, tiled=True)


def spread(value, count):
    return jnp.broadcast_to(value[None], (count,) + value.shape)


def to_tiles(value, count):
    rows, cols = value.shape
    return value.reshape(rows, count, cols // count).transpose(1, 0, 2)


def from_tiles(value):
    count, rows, cols = value.shape
    return value.transpose(1, 0, 2).reshape(rows, count * cols)


def halves(value):
    high = value.astype(BF16)
    return high, (value - high.astype(F32)).astype(BF16)


def coupling_kernel(front, place, mix_ref, couple_ref, keep_ref, send_ref):
    steps, half, lanes = keep_ref.shape[1:]
    for step in range(steps):
        width = front * lanes
        made = jnp.dot(
            mix_ref[...],
            couple_ref[:, step * width : (step + 1) * width],
            preferred_element_type=F32,
        ).astype(BF16)
        for index in range(front):
            slot = lax.rem(index - place[0] + front, front)
            piece = made[:, index * lanes : (index + 1) * lanes]
            keep_ref[slot, step] = piece[:half]
            send_ref[slot, step] = piece[half:]


def coupling(mix, couple_up, place, front, group):
    basis, border = mix.shape
    lanes = couple_up.shape[1] // (front * group)
    chunk = 4
    shape = jax.ShapeDtypeStruct((front, group, basis // 2, lanes), BF16)
    spec = pl.BlockSpec((front, chunk, basis // 2, lanes), lambda i, place: (0, i, 0, 0))
    return pl.pallas_call(
        functools.partial(coupling_kernel, front),
        out_shape=(shape, shape),
        grid_spec=pltpu.PrefetchScalarGridSpec(
            num_scalar_prefetch=1,
            grid=(group // chunk,),
            in_specs=[
                pl.BlockSpec((basis, border), lambda i, place: (0, 0)),
                pl.BlockSpec((border, chunk * front * lanes), lambda i, place: (0, i)),
            ],
            out_specs=(spec, spec),
        ),
        cost_estimate=pl.CostEstimate(
            flops=2 * basis * border * couple_up.shape[1],
            bytes_accessed=2 * couple_up.size + 2 * basis * couple_up.shape[1],
            transcendentals=0,
        ),
        name="coupling",
    )(place, mix, couple_up)


def shards(
    rhs_sub,
    rhs_sep,
    live_rows,
    lower_inv,
    upper_inv,
    couple_low,
    couple_up,
    sep_lower_inv,
    sep_upper_inv,
    basis_sub,
    basis_sep,
):
    vecs, rows = rhs_sub.shape
    blocks, block, _ = lower_inv.shape
    border = couple_low.shape[0]
    basis = basis_sub.shape[0]
    own = rhs_sep.shape[1]
    group = lax.axis_size("y") * lax.axis_size("z")
    front = lax.axis_size("x")
    cores = lax.axis_size("c")
    core = lax.axis_index("c")
    place = lax.axis_index("x")
    share = 1.0 / front
    half = basis // 2

    shaped = rhs_sub.astype(BF16).reshape(vecs, blocks, block)
    first = jnp.dot(shaped[:, 0], lower_inv[0], preferred_element_type=F32)
    border_rows = first[:, :border].astype(BF16)
    part = jnp.dot(border_rows, couple_low, preferred_element_type=F32).astype(BF16)
    got = exchange(to_tiles(part, group), YZ).astype(F32).sum(0)
    got = jnp.repeat(to_tiles(got, cores), front, axis=0)
    top_rhs = rhs_sep - exchange(got, CX).sum(0)

    mix = lax.dot_general(
        basis_sub[:, :block], upper_inv[0, :border].astype(F32), BY_LAST, precision=HIGH
    )
    mix = jnp.where(core == 0, mix, jnp.roll(mix, half, axis=0)).astype(BF16)
    keep, send = coupling(mix, couple_up, place.reshape(1), front, group)
    taken = swap_core(send)
    slots = [(keep[s].astype(F32) + taken[s].astype(F32)).astype(BF16) for s in range(front)]
    moved = [
        lax.ppermute(slots[s], "x", [(i, (i + s) % front) for i in range(front)])
        for s in range(1, front)
    ]
    reach = slots[0].astype(F32)
    for other in moved:
        reach = reach + other.astype(F32)
    reach = reach.astype(BF16)

    gram = lax.dot_general(basis_sub, basis_sub, BY_LAST, precision=HIGH)
    gram = gram + share * lax.dot_general(basis_sep, basis_sep, BY_LAST, precision=HIGH)
    lanes = sep_lower_inv.shape[1] // group
    gram = jnp.pad(gram, ((0, group * vecs - basis), (0, lanes - basis)))
    gram = gram.reshape(group, vecs, lanes)

    lower_part = jnp.dot(top_rhs.astype(BF16), sep_lower_inv, preferred_element_type=F32)
    pack = jnp.concatenate([to_tiles(lower_part, group), gram], axis=2)
    got = exchange(pack, YZ).sum(0)
    got = got + swap_core(got)
    gram_tile = got[:, lanes:]
    mine = got[:, :lanes].astype(BF16)
    pack = jnp.concatenate([spread(mine, group), reach], axis=1)
    got = exchange(pack, YZ)
    reach = got[:, vecs:].astype(F32).sum(0)
    top_lower = from_tiles(got[:, :vecs])
    upper_part = lax.dot_general(top_lower, sep_upper_inv, BY_LAST, preferred_element_type=F32)
    pack = jnp.concatenate([upper_part, gram_tile], axis=1)
    got = exchange(spread(pack, cores * front), CX)
    got = got.reshape(cores, front, vecs, own + lanes).sum(1)
    pair = jnp.concatenate([got[i, :, :own] for i in range(cores)], axis=1)
    top_sol = jnp.where(core == 0, pair[:, :own], pair[:, own:])
    gram_tile = got[0, :, own : own + basis]

    live = lax.broadcasted_iota(jnp.int32, (1, blocks, 1), 1) * block < live_rows[0]
    lower = jnp.einsum("vkr,krc->vkc", shaped, lower_inv, preferred_element_type=F32)
    lower = jnp.where(live, lower, 0.0)
    upper = jnp.einsum("vkr,krc->vkc", lower.astype(BF16), upper_inv, preferred_element_type=F32)
    upper = jnp.where(live, upper, 0.0).reshape(vecs, rows)
    coef = lax.dot_general(upper, basis_sub, BY_LAST, precision=HIGH)

    coef = coef + share * lax.dot_general(top_sol, basis_sep, BY_LAST, precision=HIGH)
    window = lax.dynamic_slice(pair, (0, place * lanes), (vecs, lanes))
    piece = lax.dot_general(window, reach, BY_LAST, precision=HIGH)
    zero = jnp.zeros_like(piece)
    coef = coef - jnp.concatenate(
        [jnp.where(core == 0, piece, zero), jnp.where(core == 0, zero, piece)], axis=1
    )
    filler = jnp.zeros((vecs, lanes - 2 * basis), BF16)
    pack = jnp.concatenate(
        [pair.astype(BF16), *halves(coef), filler, *halves(gram_tile), filler], axis=1
    )
    got = exchange(spread(pack, group), YZ)
    wide = cores * own
    full = from_tiles(got[:, :, :wide])
    coef = got[:, :, wide : wide + 2 * basis].astype(F32).sum(0)
    coef = coef[:, :basis] + coef[:, basis:]
    coef = jnp.pad(coef, ((0, 0), (0, lanes - basis)))
    coef = exchange(spread(coef, cores * front), CX).sum(0)[:, :basis]
    gram = got[: basis // vecs, :, wide + lanes : wide + lanes + 2 * basis].astype(F32)
    gram = (gram[:, :, :basis] + gram[:, :, basis:]).reshape(basis, basis)

    correction = lax.dot_general(full, couple_up, BY_LAST, preferred_element_type=F32)
    updated = jnp.concatenate([first[:, :border] - correction, first[:, border:]], axis=1)
    head = jnp.dot(updated.astype(BF16), upper_inv[0], preferred_element_type=F32)
    upper_sol = jnp.concatenate([head, upper[:, block:]], axis=1)

    coef = 2.0 * coef - jnp.dot(coef, gram, precision=HIGH)
    orth_sub = upper_sol - jnp.dot(coef, basis_sub, precision=HIGH)
    orth_sep = top_sol - jnp.dot(coef, basis_sep, precision=HIGH)
    return (orth_sub, orth_sep, coef.T)


def solution(mesh):
    split = Mesh(mesh.devices.reshape(4, 8, 2, 4), ("y", "z", "c", "x"))
    leaf = ("y", "z", "c")
    every = ("y", "z", "c", "x")
    return jax.shard_map(
        shards,
        mesh=split,
        in_specs=(
            P(None, every),
            P(None, leaf),
            P(every),
            P(every, None, None),
            P(every, None, None),
            P(every, None),
            P(every, None),
            P(leaf, "x"),
            P(leaf, "x"),
            P(None, every),
            P(None, leaf),
        ),
        out_specs=(P(None, every), P(None, leaf), P()),
        check_vma=False,
    )
```

```python
import functools

import jax
import jax.numpy as jnp
from jax import lax
from jax.experimental import pallas as pl
from jax.experimental.pallas import tpu as pltpu
from jax.sharding import Mesh, PartitionSpec as P


HIGH = lax.Precision.HIGHEST
F32 = jnp.float32
BF16 = jnp.bfloat16
YZ = ("y", "z")
CX = ("c", "x")
BY_LAST = (((1,), (1,)), ((), ()))


def swap_core(value):
    return lax.ppermute(value, "c", [(0, 1), (1, 0)])


def exchange(value, axes):
    return lax.all_to_all(value, axes, 0, 0, tiled=True)


def spread(value, count):
    return jnp.broadcast_to(value[None], (count,) + value.shape)


def to_tiles(value, count):
    rows, cols = value.shape
    return value.reshape(rows, count, cols // count).transpose(1, 0, 2)


def from_tiles(value):
    count, rows, cols = value.shape
    return value.transpose(1, 0, 2).reshape(rows, count * cols)


def halves(value):
    high = value.astype(BF16)
    return high, (value - high.astype(F32)).astype(BF16)


def coupling_kernel(front, place, mix_ref, couple_ref, keep_ref, send_ref):
    steps, half, lanes = keep_ref.shape[1:]
    for step in range(steps):
        width = front * lanes
        made = jnp.dot(
            mix_ref[...],
            couple_ref[:, step * width : (step + 1) * width],
            preferred_element_type=F32,
        ).astype(BF16)
        for index in range(front):
            slot = lax.rem(index - place[0] + front, front)
            piece = made[:, index * lanes : (index + 1) * lanes]
            keep_ref[slot, step] = piece[:half]
            send_ref[slot, step] = piece[half:]


def coupling(mix, couple_up, place, front, group):
    basis, border = mix.shape
    lanes = couple_up.shape[1] // (front * group)
    chunk = group // 2
    shape = jax.ShapeDtypeStruct((front, group, basis // 2, lanes), BF16)
    spec = pl.BlockSpec((front, chunk, basis // 2, lanes), lambda i, place: (0, i, 0, 0))
    return pl.pallas_call(
        functools.partial(coupling_kernel, front),
        out_shape=(shape, shape),
        grid_spec=pltpu.PrefetchScalarGridSpec(
            num_scalar_prefetch=1,
            grid=(group // chunk,),
            in_specs=[
                pl.BlockSpec((basis, border), lambda i, place: (0, 0)),
                pl.BlockSpec((border, chunk * front * lanes), lambda i, place: (0, i)),
            ],
            out_specs=(spec, spec),
        ),
        cost_estimate=pl.CostEstimate(
            flops=2 * basis * border * couple_up.shape[1],
            bytes_accessed=2 * couple_up.size + 2 * basis * couple_up.shape[1],
            transcendentals=0,
        ),
        compiler_params=pltpu.CompilerParams(vmem_limit_bytes=16 << 20),
        name="coupling",
    )(place, mix, couple_up)


def solve(
    rhs_sub,
    rhs_sep,
    live_rows,
    lower_inv,
    upper_inv,
    couple_low,
    couple_up,
    sep_lower_inv,
    sep_upper_inv,
    basis_sub,
    basis_sep,
):
    vecs, rows = rhs_sub.shape
    blocks, block, _ = lower_inv.shape
    border = couple_low.shape[0]
    basis = basis_sub.shape[0]
    own = rhs_sep.shape[1]
    group = lax.axis_size("y") * lax.axis_size("z")
    front = lax.axis_size("x")
    cores = lax.axis_size("c")
    core = lax.axis_index("c")
    place = lax.axis_index("x")
    share = 1.0 / front
    half = basis // 2

    shaped = rhs_sub.astype(BF16).reshape(vecs, blocks, block)
    first = jnp.dot(rhs_sub[:, :block].astype(BF16), lower_inv[0], preferred_element_type=F32)
    border_rows = first[:, :border].astype(BF16)
    part = jnp.dot(border_rows, couple_low, preferred_element_type=F32).astype(BF16)
    got = exchange(to_tiles(part, group), YZ).astype(F32).sum(0)

    mix = lax.dot_general(
        basis_sub[:, :block], upper_inv[0, :border].astype(F32), BY_LAST, precision=HIGH
    )
    mix = jnp.where(core == 0, mix, jnp.roll(mix, half, axis=0)).astype(BF16)
    keep, send = coupling(mix, couple_up, place.reshape(1), front, group)
    taken = swap_core(send)
    slots = [(keep[s].astype(F32) + taken[s].astype(F32)).astype(BF16) for s in range(front)]
    got = jnp.repeat(to_tiles(got, cores), front, axis=0)
    top_rhs = rhs_sep - exchange(got, CX).sum(0)
    lower_part = jnp.dot(top_rhs.astype(BF16), sep_lower_inv, preferred_element_type=F32)
    moved = [
        lax.ppermute(slots[s], "x", [(i, (i + s) % front) for i in range(front)])
        for s in range(1, front)
    ]
    reach = slots[0].astype(F32)
    for other in moved:
        reach = reach + other.astype(F32)
    reach = reach.astype(BF16)

    gram = lax.dot_general(basis_sub, basis_sub, BY_LAST, precision=HIGH)
    gram = gram + share * lax.dot_general(basis_sep, basis_sep, BY_LAST, precision=HIGH)
    lanes = sep_lower_inv.shape[1] // group
    gram = jnp.pad(gram, ((0, group * vecs - basis), (0, lanes - basis)))
    gram = gram.reshape(group, vecs, lanes)

    pack = jnp.concatenate([to_tiles(lower_part, group), gram], axis=2)
    got = exchange(pack, YZ).sum(0)
    got = got + swap_core(got)
    gram_tile = got[:, lanes:]
    mine = got[:, :lanes].astype(BF16)
    pack = jnp.concatenate([spread(mine, group), reach], axis=1)
    got = exchange(pack, YZ)
    reach = got[:, vecs:].astype(F32).sum(0)
    top_lower = from_tiles(got[:, :vecs])
    upper_part = lax.dot_general(top_lower, sep_upper_inv, BY_LAST, preferred_element_type=F32)
    pack = jnp.concatenate([upper_part, gram_tile], axis=1)
    got = exchange(spread(pack, cores * front), CX)
    got = got.reshape(cores, front, vecs, own + lanes).sum(1)
    pair = jnp.concatenate([got[i, :, :own] for i in range(cores)], axis=1)
    top_sol = jnp.where(core == 0, pair[:, :own], pair[:, own:])
    gram_tile = got[0, :, own : own + basis]

    live = lax.broadcasted_iota(jnp.int32, (1, blocks, 1), 1) * block < live_rows[0]
    lower = jnp.einsum("vkr,krc->vkc", shaped, lower_inv, preferred_element_type=F32)
    lower = jnp.where(live, lower, 0.0)
    upper = jnp.einsum("vkr,krc->vkc", lower.astype(BF16), upper_inv, preferred_element_type=F32)
    upper = jnp.where(live, upper, 0.0).reshape(vecs, rows)
    coef = lax.dot_general(upper, basis_sub, BY_LAST, precision=HIGH)

    coef = coef + share * lax.dot_general(top_sol, basis_sep, BY_LAST, precision=HIGH)
    window = lax.dynamic_slice(pair, (0, place * lanes), (vecs, lanes))
    piece = lax.dot_general(window, reach, BY_LAST, precision=HIGH)
    zero = jnp.zeros_like(piece)
    coef = coef - jnp.concatenate(
        [jnp.where(core == 0, piece, zero), jnp.where(core == 0, zero, piece)], axis=1
    )
    filler = jnp.zeros((vecs, lanes - 2 * basis), BF16)
    pack = jnp.concatenate(
        [pair.astype(BF16), *halves(coef), filler, *halves(gram_tile), filler], axis=1
    )
    got = exchange(spread(pack, group), YZ)
    wide = cores * own
    full = from_tiles(got[:, :, :wide])
    coef = got[:, :, wide : wide + 2 * basis].astype(F32).sum(0)
    coef = coef[:, :basis] + coef[:, basis:]
    coef = jnp.pad(coef, ((0, 0), (0, lanes - basis)))
    coef = exchange(spread(coef, cores * front), CX).sum(0)[:, :basis]
    gram = got[: basis // vecs, :, wide + lanes : wide + lanes + 2 * basis].astype(F32)
    gram = (gram[:, :, :basis] + gram[:, :, basis:]).reshape(basis, basis)

    correction = lax.dot_general(full, couple_up, BY_LAST, preferred_element_type=F32)
    updated = jnp.concatenate([first[:, :border] - correction, first[:, border:]], axis=1)
    head = jnp.dot(updated.astype(BF16), upper_inv[0], preferred_element_type=F32)
    upper_sol = jnp.concatenate([head, upper[:, block:]], axis=1)

    coef = 2.0 * coef - jnp.dot(coef, gram, precision=HIGH)
    orth_sub = upper_sol - jnp.dot(coef, basis_sub, precision=HIGH)
    orth_sep = top_sol - jnp.dot(coef, basis_sep, precision=HIGH)
    return (orth_sub, orth_sep, coef.T)


def solution(mesh):
    split = Mesh(mesh.devices.reshape(4, 8, 2, 4), ("y", "z", "c", "x"))
    leaf = ("y", "z", "c")
    every = ("y", "z", "c", "x")
    return jax.shard_map(
        solve,
        mesh=split,
        in_specs=(
            P(None, every),
            P(None, leaf),
            P(every),
            P(every, None, None),
            P(every, None, None),
            P(every, None),
            P(every, None),
            P(leaf, "x"),
            P(leaf, "x"),
            P(None, every),
            P(None, leaf),
        ),
        out_specs=(P(None, every), P(None, leaf), P()),
        check_vma=False,
    )
```

```python
import jax
import jax.numpy as jnp
from jax import lax
from jax.sharding import Mesh, PartitionSpec as P


HIGH = lax.Precision.HIGHEST
F32 = jnp.float32
BF16 = jnp.bfloat16
BY_LAST = (((1,), (1,)), ((), ()))


def swap_core(value):
    return lax.ppermute(value, "c", [(0, 1), (1, 0)])


def sum_front(value):
    count = lax.axis_size("x")
    moved = [
        lax.ppermute(value, "x", [(i, (i + step) % count) for i in range(count)])
        for step in range(1, count)
    ]
    for other in moved:
        value = value + other
    return value


def exchange(value):
    return lax.all_to_all(value, ("y", "z"), 0, 0, tiled=True)


def spread(value, count):
    return jnp.broadcast_to(value[None], (count,) + value.shape)


def to_tiles(value, count):
    rows, cols = value.shape
    return value.reshape(rows, count, cols // count).transpose(1, 0, 2)


def from_tiles(value):
    count, rows, cols = value.shape
    return value.transpose(1, 0, 2).reshape(rows, count * cols)


def solve(
    rhs_sub,
    rhs_sep,
    live_rows,
    lower_inv,
    upper_inv,
    couple_low,
    couple_up,
    sep_lower_inv,
    sep_upper_inv,
    basis_sub,
    basis_sep,
):
    vecs, rows = rhs_sub.shape
    blocks, block, _ = lower_inv.shape
    border = couple_low.shape[0]
    basis = basis_sub.shape[0]
    own = rhs_sep.shape[1]
    group = lax.axis_size("y") * lax.axis_size("z")
    share = 1.0 / lax.axis_size("x")
    core = lax.axis_index("c")

    first = jnp.dot(rhs_sub[:, :block].astype(BF16), lower_inv[0], preferred_element_type=F32)
    border_rows = first[:, :border].astype(BF16)
    part = jnp.dot(border_rows, couple_low, preferred_element_type=F32)
    part = to_tiles(part, 2 * group).reshape(group, 2, vecs, own)
    keep = jnp.where(core == 0, part[:, 0], part[:, 1])
    send = jnp.where(core == 0, part[:, 1], part[:, 0]).astype(BF16)
    pack = (keep + swap_core(send).astype(F32)).astype(BF16)
    top_rhs = rhs_sep - sum_front(exchange(pack).astype(F32).sum(0))

    gram = lax.dot_general(basis_sub, basis_sub, BY_LAST, precision=HIGH)
    gram = gram + share * lax.dot_general(basis_sep, basis_sep, BY_LAST, precision=HIGH)
    gram = gram + swap_core(gram)
    high = gram.astype(BF16)
    low = (gram - high.astype(F32)).astype(BF16)
    lanes = sep_lower_inv.shape[1] // group
    gram = jnp.concatenate([high, low], axis=1)
    gram = jnp.pad(gram, ((0, group * vecs - basis), (0, lanes - 2 * basis)))
    gram = gram.reshape(group, vecs, lanes)
    mix = lax.dot_general(
        basis_sub[:, :block], upper_inv[0, :border].astype(F32), BY_LAST, precision=HIGH
    )

    live = lax.broadcasted_iota(jnp.int32, (1, blocks, 1), 1) * block < live_rows[0]
    shaped = lax.optimization_barrier(rhs_sub).astype(BF16).reshape(vecs, blocks, block)
    lower = jnp.einsum("vkr,krc->vkc", shaped, lower_inv, preferred_element_type=F32)
    lower = jnp.where(live, lower, 0.0)
    upper = jnp.einsum("vkr,krc->vkc", lower.astype(BF16), upper_inv, preferred_element_type=F32)
    upper = jnp.where(live, upper, 0.0).reshape(vecs, rows)
    coef = lax.dot_general(upper, basis_sub, BY_LAST, precision=HIGH)

    lower_part = jnp.dot(top_rhs.astype(BF16), sep_lower_inv, preferred_element_type=F32)
    lower_part = lower_part + swap_core(lower_part)
    mine = exchange(to_tiles(lower_part, group)).sum(0).astype(BF16)
    got = exchange(jnp.concatenate([spread(mine, group), gram], axis=1))
    gram = got[:, vecs:].astype(F32).sum(0)
    gram = gram[:, :basis] + gram[:, basis : 2 * basis]
    top_lower = from_tiles(got[:, :vecs])
    upper_part = lax.dot_general(top_lower, sep_upper_inv, BY_LAST, preferred_element_type=F32)
    got = sum_front(jnp.concatenate([upper_part, gram], axis=1))
    top_sol = got[:, :own]
    gram = got[:, own:]

    mine = exchange(spread(top_sol.astype(BF16), group))
    other = swap_core(mine)
    full = jnp.stack(
        [jnp.where(core == 0, mine, other), jnp.where(core == 0, other, mine)], axis=1
    )
    full = from_tiles(full.reshape(2 * group, vecs, own))
    correction = lax.dot_general(full, couple_up, BY_LAST, preferred_element_type=F32)

    coef = coef + share * lax.dot_general(top_sol, basis_sep, BY_LAST, precision=HIGH)
    coef = coef - lax.dot_general(correction, mix, BY_LAST, precision=HIGH)
    gap = jnp.zeros((vecs, lanes // 2 - basis), F32)
    coef = sum_front(coef + swap_core(coef))
    pack = jnp.concatenate([coef, gap, gram, gap], axis=1)
    got = exchange(spread(pack, group))
    coef = got[:, :, :basis].sum(0)
    gram = got[: basis // vecs, :, lanes // 2 : lanes // 2 + basis].reshape(basis, basis)

    updated = jnp.concatenate([first[:, :border] - correction, first[:, border:]], axis=1)
    head = jnp.dot(updated.astype(BF16), upper_inv[0], preferred_element_type=F32)
    upper_sol = jnp.concatenate([head, upper[:, block:]], axis=1)

    coef = 2.0 * coef - jnp.dot(coef, gram, precision=HIGH)
    orth_sub = upper_sol - jnp.dot(coef, basis_sub, precision=HIGH)
    orth_sep = top_sol - jnp.dot(coef, basis_sep, precision=HIGH)
    return (orth_sub, orth_sep, coef.T)


def solution(mesh):
    split = Mesh(mesh.devices.reshape(4, 8, 2, 4), ("y", "z", "c", "x"))
    leaf = ("y", "z", "c")
    every = ("y", "z", "c", "x")
    return jax.shard_map(
        solve,
        mesh=split,
        in_specs=(
            P(None, every),
            P(None, leaf),
            P(every),
            P(every, None, None),
            P(every, None, None),
            P(every, None),
            P(every, None),
            P(leaf, "x"),
            P(leaf, "x"),
            P(None, every),
            P(None, leaf),
        ),
        out_specs=(P(None, every), P(None, leaf), P()),
        check_vma=False,
    )
```

```python
import jax
import jax.numpy as jnp
from jax import lax
from jax.experimental import pallas as pl
from jax.experimental.pallas import tpu as pltpu
from jax.sharding import Mesh, PartitionSpec as P


HIGH = lax.Precision.HIGHEST
F32 = jnp.float32
BF16 = jnp.bfloat16
BY_LAST = (((1,), (1,)), ((), ()))


def swap_core(value):
    return lax.ppermute(value, "c", [(0, 1), (1, 0)])


def sum_front(value):
    count = lax.axis_size("x")
    moved = [
        lax.ppermute(value, "x", [(i, (i + step) % count) for i in range(count)])
        for step in range(1, count)
    ]
    for other in moved:
        value = value + other
    return value


def exchange(value):
    return lax.all_to_all(value, ("y", "z"), 0, 0, tiled=True)


def spread(value, count):
    return jnp.broadcast_to(value[None], (count,) + value.shape)


def to_tiles(value, count):
    rows, cols = value.shape
    return value.reshape(rows, count, cols // count).transpose(1, 0, 2)


def from_tiles(value):
    count, rows, cols = value.shape
    return value.transpose(1, 0, 2).reshape(rows, count * cols)


def finish_kernel(got_ref, upper_ref, head_ref, top_ref, sub_ref, sep_ref, *outs):
    sub_out, sep_out, coef_out = outs
    basis = sub_ref.shape[0]
    vecs, own = head_ref.shape
    middle = got_ref.shape[2] // 2
    coef = got_ref[0]
    for index in range(1, got_ref.shape[0]):
        coef = coef + got_ref[index]
    coef = coef[:, :basis]
    gram = got_ref[: basis // vecs].reshape(basis, 2 * middle)[:, middle : middle + basis]
    coef = 2.0 * coef - jnp.dot(coef, gram, precision=HIGH, preferred_element_type=F32)
    coef_out[...] = coef
    sep_out[...] = top_ref[:, :own] - jnp.dot(
        coef, sep_ref[...], precision=HIGH, preferred_element_type=F32
    )
    moved = jnp.dot(coef, sub_ref[...], precision=HIGH, preferred_element_type=F32)
    sub_out[:, :own] = head_ref[...] - moved[:, :own]
    sub_out[:, own:] = upper_ref[:, own:] - moved[:, own:]


def finish(got, upper, head, top_sol, basis_sub, basis_sep):
    basis, rows = basis_sub.shape
    vecs, own = head.shape
    return pl.pallas_call(
        finish_kernel,
        out_shape=(
            jax.ShapeDtypeStruct((vecs, rows), F32),
            jax.ShapeDtypeStruct((vecs, own), F32),
            jax.ShapeDtypeStruct((vecs, basis), F32),
        ),
        compiler_params=pltpu.CompilerParams(vmem_limit_bytes=8 << 20),
        cost_estimate=pl.CostEstimate(
            flops=2 * vecs * basis * rows,
            bytes_accessed=4 * (basis_sub.size + 2 * upper.size),
            transcendentals=0,
        ),
        name="finish",
    )(got, upper, head, top_sol, basis_sub, basis_sep)


def solve(
    rhs_sub,
    rhs_sep,
    live_rows,
    lower_inv,
    upper_inv,
    couple_low,
    couple_up,
    sep_lower_inv,
    sep_upper_inv,
    basis_sub,
    basis_sep,
):
    vecs, rows = rhs_sub.shape
    blocks, block, _ = lower_inv.shape
    border = couple_low.shape[0]
    basis = basis_sub.shape[0]
    own = rhs_sep.shape[1]
    group = lax.axis_size("y") * lax.axis_size("z")
    share = 1.0 / lax.axis_size("x")
    core = lax.axis_index("c")

    first = jnp.dot(rhs_sub[:, :block].astype(BF16), lower_inv[0], preferred_element_type=F32)
    border_rows = first[:, :border].astype(BF16)
    part = jnp.dot(border_rows, couple_low, preferred_element_type=F32)
    part = to_tiles(part, 2 * group).reshape(group, 2, vecs, own)
    keep = jnp.where(core == 0, part[:, 0], part[:, 1])
    send = jnp.where(core == 0, part[:, 1], part[:, 0]).astype(BF16)
    pack = (keep + swap_core(send).astype(F32)).astype(BF16)
    top_rhs = rhs_sep - sum_front(exchange(pack).astype(F32).sum(0))

    gram = lax.dot_general(basis_sub, basis_sub, BY_LAST, precision=HIGH)
    gram = gram + share * lax.dot_general(basis_sep, basis_sep, BY_LAST, precision=HIGH)
    gram = gram + swap_core(gram)
    high = gram.astype(BF16)
    low = (gram - high.astype(F32)).astype(BF16)
    lanes = sep_lower_inv.shape[1] // group
    gram = jnp.concatenate([high, low], axis=1)
    gram = jnp.pad(gram, ((0, group * vecs - basis), (0, lanes - 2 * basis)))
    gram = gram.reshape(group, vecs, lanes)
    mix = lax.dot_general(
        basis_sub[:, :block], upper_inv[0, :border].astype(F32), BY_LAST, precision=HIGH
    )

    live = lax.broadcasted_iota(jnp.int32, (1, blocks, 1), 1) * block < live_rows[0]
    shaped = lax.optimization_barrier(rhs_sub).astype(BF16).reshape(vecs, blocks, block)
    lower = jnp.einsum("vkr,krc->vkc", shaped, lower_inv, preferred_element_type=F32)
    lower = jnp.where(live, lower, 0.0)
    upper = jnp.einsum("vkr,krc->vkc", lower.astype(BF16), upper_inv, preferred_element_type=F32)
    upper = jnp.where(live, upper, 0.0).reshape(vecs, rows)
    coef = lax.dot_general(upper, basis_sub, BY_LAST, precision=HIGH)

    lower_part = jnp.dot(top_rhs.astype(BF16), sep_lower_inv, preferred_element_type=F32)
    lower_part = lower_part + swap_core(lower_part)
    mine = exchange(to_tiles(lower_part, group)).sum(0).astype(BF16)
    got = exchange(jnp.concatenate([spread(mine, group), gram], axis=1))
    gram = got[:, vecs:].astype(F32).sum(0)
    gram = gram[:, :basis] + gram[:, basis : 2 * basis]
    top_lower = from_tiles(got[:, :vecs])
    upper_part = lax.dot_general(top_lower, sep_upper_inv, BY_LAST, preferred_element_type=F32)
    top_all = sum_front(jnp.concatenate([upper_part, gram], axis=1))
    top_sol = top_all[:, :own]
    gram = top_all[:, own:]

    mine = exchange(spread(top_sol.astype(BF16), group))
    other = swap_core(mine)
    full = jnp.stack(
        [jnp.where(core == 0, mine, other), jnp.where(core == 0, other, mine)], axis=1
    )
    full = from_tiles(full.reshape(2 * group, vecs, own))
    correction = lax.dot_general(full, couple_up, BY_LAST, preferred_element_type=F32)

    coef = coef + share * lax.dot_general(top_sol, basis_sep, BY_LAST, precision=HIGH)
    coef = coef - lax.dot_general(correction, mix, BY_LAST, precision=HIGH)
    gap = jnp.zeros((vecs, lanes // 2 - basis), F32)
    coef = sum_front(coef + swap_core(coef))
    pack = jnp.concatenate([coef, gap, gram, gap], axis=1)
    got = exchange(spread(pack, group))
    updated = jnp.concatenate([first[:, :border] - correction, first[:, border:]], axis=1)
    head = jnp.dot(updated.astype(BF16), upper_inv[0], preferred_element_type=F32)

    orth_sub, orth_sep, coef = finish(got, upper, head, top_all, basis_sub, basis_sep)
    return (orth_sub, orth_sep, coef.T)


def solution(mesh):
    split = Mesh(mesh.devices.reshape(4, 8, 2, 4), ("y", "z", "c", "x"))
    leaf = ("y", "z", "c")
    every = ("y", "z", "c", "x")
    return jax.shard_map(
        solve,
        mesh=split,
        in_specs=(
            P(None, every),
            P(None, leaf),
            P(every),
            P(every, None, None),
            P(every, None, None),
            P(every, None),
            P(every, None),
            P(leaf, "x"),
            P(leaf, "x"),
            P(None, every),
            P(None, leaf),
        ),
        out_specs=(P(None, every), P(None, leaf), P()),
        check_vma=False,
    )
```

```python
import jax
import jax.numpy as jnp
from jax import lax
from jax.experimental import pallas as pl
from jax.experimental.pallas import tpu as pltpu
from jax.sharding import Mesh, PartitionSpec as P


HIGH = lax.Precision.HIGHEST
F32 = jnp.float32
BF16 = jnp.bfloat16
BY_LAST = (((1,), (1,)), ((), ()))


def swap_core(value):
    return lax.ppermute(value, "c", [(0, 1), (1, 0)])


def sum_front(value):
    count = lax.axis_size("x")
    moved = [
        lax.ppermute(value, "x", [(i, (i + step) % count) for i in range(count)])
        for step in range(1, count)
    ]
    for other in moved:
        value = value + other
    return value


def exchange(value):
    return lax.all_to_all(value, ("y", "z"), 0, 0, tiled=True)


def spread(value, count):
    return jnp.broadcast_to(value[None], (count,) + value.shape)


def to_tiles(value, count):
    rows, cols = value.shape
    return value.reshape(rows, count, cols // count).transpose(1, 0, 2)


def from_tiles(value):
    count, rows, cols = value.shape
    return value.transpose(1, 0, 2).reshape(rows, count * cols)


def stream(weight_hbm, buffer, done):
    width = weight_hbm.shape[1] // done.shape[0]
    copies = []
    for index in range(done.shape[0]):
        part = pl.ds(index * width, width)
        copies.append(
            pltpu.make_async_copy(weight_hbm.at[:, part], buffer.at[:, part], done.at[index])
        )
    for copy in copies:
        copy.start()
    return copies, width


def lower_kernel(left_ref, weight_hbm, out_ref, buffer, done):
    copies, width = stream(weight_hbm, buffer, done)
    for index, copy in enumerate(copies):
        part = slice(index * width, (index + 1) * width)
        copy.wait()
        out_ref[:, part] = jnp.dot(left_ref[...], buffer[:, part], preferred_element_type=F32)


def weighted(kernel, left, weight, shape):
    return pl.pallas_call(
        kernel,
        out_shape=jax.ShapeDtypeStruct(shape, F32),
        in_specs=[
            pl.BlockSpec(memory_space=pltpu.MemorySpace.VMEM),
            pl.BlockSpec(memory_space=pltpu.MemorySpace.HBM),
        ],
        out_specs=pl.BlockSpec(memory_space=pltpu.MemorySpace.VMEM),
        scratch_shapes=[pltpu.VMEM(weight.shape, weight.dtype), pltpu.SemaphoreType.DMA((8,))],
        compiler_params=pltpu.CompilerParams(vmem_limit_bytes=52 << 20),
        cost_estimate=pl.CostEstimate(
            flops=16 * weight.size, bytes_accessed=2 * weight.size, transcendentals=0
        ),
    )(left, weight)


def finish_kernel(got_ref, upper_ref, head_ref, top_ref, sub_ref, sep_ref, *outs):
    sub_out, sep_out, coef_out = outs
    basis = sub_ref.shape[0]
    vecs, own = head_ref.shape
    middle = got_ref.shape[2] // 2
    coef = got_ref[0]
    for index in range(1, got_ref.shape[0]):
        coef = coef + got_ref[index]
    coef = coef[:, :basis]
    gram = got_ref[: basis // vecs].reshape(basis, 2 * middle)[:, middle : middle + basis]
    coef = 2.0 * coef - jnp.dot(coef, gram, precision=HIGH, preferred_element_type=F32)
    coef_out[...] = coef
    sep_out[...] = top_ref[:, :own] - jnp.dot(
        coef, sep_ref[...], precision=HIGH, preferred_element_type=F32
    )
    moved = jnp.dot(coef, sub_ref[...], precision=HIGH, preferred_element_type=F32)
    sub_out[:, :own] = head_ref[...] - moved[:, :own]
    sub_out[:, own:] = upper_ref[:, own:] - moved[:, own:]


def finish(got, upper, head, top_sol, basis_sub, basis_sep):
    basis, rows = basis_sub.shape
    vecs, own = head.shape
    return pl.pallas_call(
        finish_kernel,
        out_shape=(
            jax.ShapeDtypeStruct((vecs, rows), F32),
            jax.ShapeDtypeStruct((vecs, own), F32),
            jax.ShapeDtypeStruct((vecs, basis), F32),
        ),
        compiler_params=pltpu.CompilerParams(vmem_limit_bytes=8 << 20),
        cost_estimate=pl.CostEstimate(
            flops=2 * vecs * basis * rows,
            bytes_accessed=4 * (basis_sub.size + 2 * upper.size),
            transcendentals=0,
        ),
        name="finish",
    )(got, upper, head, top_sol, basis_sub, basis_sep)


def solve(
    rhs_sub,
    rhs_sep,
    live_rows,
    lower_inv,
    upper_inv,
    couple_low,
    couple_up,
    sep_lower_inv,
    sep_upper_inv,
    basis_sub,
    basis_sep,
):
    vecs, rows = rhs_sub.shape
    blocks, block, _ = lower_inv.shape
    border = couple_low.shape[0]
    basis = basis_sub.shape[0]
    own = rhs_sep.shape[1]
    group = lax.axis_size("y") * lax.axis_size("z")
    share = 1.0 / lax.axis_size("x")
    core = lax.axis_index("c")

    first = jnp.dot(rhs_sub[:, :block].astype(BF16), lower_inv[0], preferred_element_type=F32)
    border_rows = first[:, :border].astype(BF16)
    part = jnp.dot(border_rows, couple_low, preferred_element_type=F32)
    part = to_tiles(part, 2 * group).reshape(group, 2, vecs, own)
    keep = jnp.where(core == 0, part[:, 0], part[:, 1])
    send = jnp.where(core == 0, part[:, 1], part[:, 0]).astype(BF16)
    pack = (keep + swap_core(send).astype(F32)).astype(BF16)
    top_rhs = rhs_sep - sum_front(exchange(pack).astype(F32).sum(0))

    gram = lax.dot_general(basis_sub, basis_sub, BY_LAST, precision=HIGH)
    gram = gram + share * lax.dot_general(basis_sep, basis_sep, BY_LAST, precision=HIGH)
    gram = gram + swap_core(gram)
    high = gram.astype(BF16)
    low = (gram - high.astype(F32)).astype(BF16)
    lanes = sep_lower_inv.shape[1] // group
    gram = jnp.concatenate([high, low], axis=1)
    gram = jnp.pad(gram, ((0, group * vecs - basis), (0, lanes - 2 * basis)))
    gram = gram.reshape(group, vecs, lanes)
    mix = lax.dot_general(
        basis_sub[:, :block], upper_inv[0, :border].astype(F32), BY_LAST, precision=HIGH
    )

    live = lax.broadcasted_iota(jnp.int32, (1, blocks, 1), 1) * block < live_rows[0]
    shaped = lax.optimization_barrier(rhs_sub).astype(BF16).reshape(vecs, blocks, block)
    lower = jnp.einsum("vkr,krc->vkc", shaped, lower_inv, preferred_element_type=F32)
    lower = jnp.where(live, lower, 0.0)
    upper = jnp.einsum("vkr,krc->vkc", lower.astype(BF16), upper_inv, preferred_element_type=F32)
    upper = jnp.where(live, upper, 0.0).reshape(vecs, rows)
    coef = lax.dot_general(upper, basis_sub, BY_LAST, precision=HIGH)

    lower_part = weighted(lower_kernel, top_rhs.astype(BF16), sep_lower_inv, (vecs, group * lanes))
    lower_part = lower_part + swap_core(lower_part)
    mine = exchange(to_tiles(lower_part, group)).sum(0).astype(BF16)
    got = exchange(jnp.concatenate([spread(mine, group), gram], axis=1))
    gram = got[:, vecs:].astype(F32).sum(0)
    gram = gram[:, :basis] + gram[:, basis : 2 * basis]
    top_lower = from_tiles(got[:, :vecs])
    upper_part = lax.dot_general(top_lower, sep_upper_inv, BY_LAST, preferred_element_type=F32)
    top_all = sum_front(jnp.concatenate([upper_part, gram], axis=1))
    top_sol = top_all[:, :own]
    gram = top_all[:, own:]

    mine = exchange(spread(top_sol.astype(BF16), group))
    other = swap_core(mine)
    full = jnp.stack(
        [jnp.where(core == 0, mine, other), jnp.where(core == 0, other, mine)], axis=1
    )
    full = from_tiles(full.reshape(2 * group, vecs, own))
    correction = lax.dot_general(full, couple_up, BY_LAST, preferred_element_type=F32)

    coef = coef + share * lax.dot_general(top_sol, basis_sep, BY_LAST, precision=HIGH)
    coef = coef - lax.dot_general(correction, mix, BY_LAST, precision=HIGH)
    gap = jnp.zeros((vecs, lanes // 2 - basis), F32)
    coef = sum_front(coef + swap_core(coef))
    pack = jnp.concatenate([coef, gap, gram, gap], axis=1)
    got = exchange(spread(pack, group))
    updated = jnp.concatenate([first[:, :border] - correction, first[:, border:]], axis=1)
    head = jnp.dot(updated.astype(BF16), upper_inv[0], preferred_element_type=F32)

    orth_sub, orth_sep, coef = finish(got, upper, head, top_all, basis_sub, basis_sep)
    return (orth_sub, orth_sep, coef.T)


def solution(mesh):
    split = Mesh(mesh.devices.reshape(4, 8, 2, 4), ("y", "z", "c", "x"))
    leaf = ("y", "z", "c")
    every = ("y", "z", "c", "x")
    return jax.shard_map(
        solve,
        mesh=split,
        in_specs=(
            P(None, every),
            P(None, leaf),
            P(every),
            P(every, None, None),
            P(every, None, None),
            P(every, None),
            P(every, None),
            P(leaf, "x"),
            P(leaf, "x"),
            P(None, every),
            P(None, leaf),
        ),
        out_specs=(P(None, every), P(None, leaf), P()),
        check_vma=False,
    )
```
